32 devices in a mesh: wide: 8 (over z, core), col: 4 (over y, x).
Axes of the slice: x: 2, y: 2, z: 4, core: 2. Of those that a mesh axis runs over, the one named last changes fastest.
Arguments:
- amplitudes: float32 [2048, 2048], P('wide', 'col'), may hold values from -6 to 6
- integrals: float32 [2048, 2048], P('wide', 'col'), may hold values from -0.125 to 0.125
Outputs:
- ladder: float32 [2048, 2048], P(('wide', 'col'))
The draws below stay inside these ranges and needn't reach their ends.
All inputs are finite; a program needn't handle non-finite values.
Results may differ from the reference program's by a relative error of at most 0.00007.
Values sent between devices are 32-bit elements; how exact they have to be, the bound alone decides.
A program may use at most 64 MiB of HBM per device.

```python
import jax
import jax.numpy as jnp
from jax import lax

IJ = 2048
CD = 2048
AB = 2048


def shard_levels(stream_key, dims, pieces, least, largest):
    def one(dim, parts):
        steps = jax.random.uniform(jax.random.fold_in(jax.random.fold_in(stream_key, 6), dim), (parts,), jnp.float32, least / len(pieces), largest / len(pieces))
        return jnp.repeat(jnp.exp(steps), dims[dim] // parts).reshape((-1,) + (1,) * (len(dims) - dim - 1))

    factor_of = one(*pieces[0])
    for cut in pieces[1:]:
        factor_of = factor_of * one(*cut)
    return factor_of


def scatter_about(own_key, extent, width, reach, shards=(), kind=jnp.bfloat16):
    entries = jax.random.normal(own_key, extent, jnp.float32) * width
    if len(shards) > 0:
        entries = shard_levels(own_key, extent, shards, -0.22, 0.18) * entries
    return jnp.clip(entries, min=-reach, max=reach).astype(kind)


def setup_inputs(seed: int = 0) -> dict:
    key_list = jax.random.split(jax.random.key(seed), 3)
    amplitudes = scatter_about(key_list[0], (IJ, CD), 1.0, 6.0, ((0, 8), (1, 4)), jnp.float32)
    integrals = scatter_about(key_list[1], (AB, CD), CD ** -0.5, 0.125, ((0, 8), (1, 4)), jnp.float32)
    return {"amplitudes": amplitudes, "integrals": integrals}


def reference(amplitudes, integrals):
    return lax.dot_general(amplitudes, integrals, (((1,), (1,)), ((), ())), precision=lax.Precision.HIGHEST, preferred_element_type=jnp.float32)
```

```python
import jax
import jax.numpy as jnp
from jax import lax
from jax.sharding import PartitionSpec as P


def on_device(amplitudes, integrals):
    panel = lax.all_gather(integrals, "wide", axis=0, tiled=True)
    part = lax.dot_general(
        amplitudes,
        panel,
        (((1,), (1,)), ((), ())),
        precision=lax.Precision.HIGHEST,
        preferred_element_type=jnp.float32,
    )
    return lax.psum_scatter(part, "col", scatter_dimension=0, tiled=True)


def solution(mesh):
    return jax.shard_map(
        on_device,
        mesh=mesh,
        in_specs=(P("wide", "col"), P("wide", "col")),
        out_specs=P(("wide", "col"), None),
        check_vma=False,
    )
```

```python
import functools

import jax
import jax.numpy as jnp
from jax import lax
from jax.experimental import pallas as pl
from jax.experimental.pallas import tpu as pltpu
from jax.sharding import PartitionSpec as P

MESH = pl.DeviceIdType.MESH
CORES = 2
PIECES = 2


def halves(x):
    high = x.astype(jnp.bfloat16)
    low = (x - high.astype(jnp.float32)).astype(jnp.bfloat16)
    return high, low


def dot(x, y):
    return lax.dot_general(x, y, (((1,), (1,)), ((), ())), preferred_element_type=jnp.float32)


def kernel(wide, cols, a_ref, b_ref, o_ref, panel, a_high, a_low, part, landed,
           send_line, send_pair, recv_panel, send_sum, recv_sum):
    w = lax.axis_index("wide")
    c = lax.axis_index("col")
    line = wide // CORES
    g = w // CORES
    core = w % CORES
    sibling = g * CORES + 1 - core
    rows = b_ref.shape[0] // PIECES
    share = o_ref.shape[0]

    barrier = pltpu.get_barrier_semaphore()

    def greet(wide_index, col_index):
        pl.semaphore_signal(barrier, inc=1, device_id={"wide": wide_index, "col": col_index}, device_id_type=MESH)

    has_left = g > 0
    has_right = g < line - 1
    pl.when(has_left)(lambda: greet(w - CORES, c))
    pl.when(has_right)(lambda: greet(w + CORES, c))
    greet(sibling, c)

    @pl.loop(1, cols)
    def _(j):
        greet(w, (c + j) % cols)

    pl.semaphore_wait(barrier, cols + has_left.astype(jnp.int32) + has_right.astype(jnp.int32))

    def push(src, slot, sem, target):
        return pltpu.make_async_remote_copy(
            src_ref=src, dst_ref=panel.at[slot], send_sem=sem, recv_sem=recv_panel.at[slot],
            device_id={"wide": target, "col": c}, device_id_type=MESH)

    def own(h):
        return b_ref.at[pl.ds(h * rows, rows)]

    def arrive(slot):
        pltpu.make_async_copy(panel.at[slot], panel.at[slot], recv_panel.at[slot]).wait()

    def contract(block, slot):
        high, low = halves(block)
        product = dot(a_high[...], high) + (dot(a_high[...], low) + dot(a_low[...], high))
        for k in range(cols):
            part[slot, k] = product[k * share:(k + 1) * share]

        @pl.loop(1, cols)
        def _(j):
            peer = (c + j) % cols
            pltpu.make_async_remote_copy(
                src_ref=part.at[slot, peer], dst_ref=landed.at[slot, cols - 1 - j],
                send_sem=send_sum.at[slot], recv_sem=recv_sum.at[slot],
                device_id={"wide": w, "col": peer}, device_id_type=MESH).start()

    for h in range(PIECES):
        slot = w * PIECES + h
        pl.when(has_right)(lambda: push(own(h), slot, send_line.at[slot], w + CORES).start())
        pl.when(has_left)(lambda: push(own(h), slot, send_line.at[wide * PIECES + h], w - CORES).start())
        push(own(h), slot, send_pair.at[slot], sibling).start()

    high, low = halves(a_ref[...])
    a_high[...] = high
    a_low[...] = low
    for h in range(PIECES):
        contract(b_ref[h * rows:(h + 1) * rows], w * PIECES + h)
    for h in range(PIECES):
        slot = sibling * PIECES + h
        arrive(slot)
        contract(panel[slot], slot)

    @pl.loop(1, line)
    def _(d):
        @pl.loop(0, PIECES)
        def _(h):
            left_slot = (w - d * CORES) * PIECES + h
            right_slot = (w + d * CORES) * PIECES + h
            pair_left = (sibling - d * CORES) * PIECES + h
            pair_right = (sibling + d * CORES) * PIECES + h

            @pl.when(g - d >= 0)
            def _():
                arrive(left_slot)
                pl.when(has_right)(lambda: push(panel.at[left_slot], left_slot, send_line.at[left_slot], w + CORES).start())
                push(panel.at[left_slot], left_slot, send_pair.at[left_slot], sibling).start()

            @pl.when(g + d < line)
            def _():
                arrive(right_slot)
                pl.when(has_left)(lambda: push(panel.at[right_slot], right_slot, send_line.at[right_slot], w - CORES).start())
                push(panel.at[right_slot], right_slot, send_pair.at[right_slot], sibling).start()

            @pl.when(g - d >= 0)
            def _():
                contract(panel[left_slot], left_slot)

            @pl.when(g + d < line)
            def _():
                contract(panel[right_slot], right_slot)

            @pl.when(g - d >= 0)
            def _():
                arrive(pair_left)
                contract(panel[pair_left], pair_left)

            @pl.when(g + d < line)
            def _():
                arrive(pair_right)
                contract(panel[pair_right], pair_right)

    @pl.loop(0, wide * PIECES)
    def _(slot):
        pltpu.make_async_copy(landed.at[slot], landed.at[slot], recv_sum.at[slot]).wait()
        total = part[slot, c]
        for k in range(cols - 1):
            total = total + landed[slot, k]
        o_ref[:, pl.ds(pl.multiple_of(slot * rows, rows), rows)] = total

    for h in range(PIECES):
        slot = w * PIECES + h
        pl.when(has_right)(lambda: push(own(h), slot, send_line.at[slot], w + CORES).wait_send())
        pl.when(has_left)(lambda: push(own(h), slot, send_line.at[wide * PIECES + h], w - CORES).wait_send())
        push(own(h), slot, send_pair.at[slot], sibling).wait_send()

    @pl.loop(1, line)
    def _(d):
        @pl.loop(0, PIECES)
        def _(h):
            left_slot = (w - d * CORES) * PIECES + h
            right_slot = (w + d * CORES) * PIECES + h

            @pl.when(g - d >= 0)
            def _():
                pl.when(has_right)(lambda: push(panel.at[left_slot], left_slot, send_line.at[left_slot], w + CORES).wait_send())
                push(panel.at[left_slot], left_slot, send_pair.at[left_slot], sibling).wait_send()

            @pl.when(g + d < line)
            def _():
                pl.when(has_left)(lambda: push(panel.at[right_slot], right_slot, send_line.at[right_slot], w - CORES).wait_send())
                push(panel.at[right_slot], right_slot, send_pair.at[right_slot], sibling).wait_send()

    @pl.loop(0, wide * PIECES)
    def _(slot):
        pltpu.make_async_copy(landed.at[slot], landed.at[slot], send_sum.at[slot]).wait()


def on_device(wide, cols, amplitudes, integrals):
    rows_a, depth = amplitudes.shape
    rows_b = integrals.shape[0]
    share = rows_a // cols
    slots = wide * PIECES
    rows = rows_b // PIECES
    vmem = pl.BlockSpec(memory_space=pltpu.VMEM)
    return pl.pallas_call(
        functools.partial(kernel, wide, cols),
        out_shape=jax.ShapeDtypeStruct((share, wide * rows_b), jnp.float32),
        in_specs=[vmem, vmem],
        out_specs=vmem,
        scratch_shapes=[
            pltpu.VMEM((slots, rows, depth), jnp.float32),
            pltpu.VMEM((rows_a, depth), jnp.bfloat16),
            pltpu.VMEM((rows_a, depth), jnp.bfloat16),
            pltpu.VMEM((slots, cols, share, rows), jnp.float32),
            pltpu.VMEM((slots, cols - 1, share, rows), jnp.float32),
            pltpu.SemaphoreType.DMA((slots + PIECES,)),
            pltpu.SemaphoreType.DMA((slots,)),
            pltpu.SemaphoreType.DMA((slots,)),
            pltpu.SemaphoreType.DMA((slots,)),
            pltpu.SemaphoreType.DMA((slots,)),
        ],
        compiler_params=pltpu.CompilerParams(
            collective_id=0, has_side_effects=True, vmem_limit_bytes=56 * 1024 * 1024),
    )(amplitudes, integrals)


def solution(mesh):
    return jax.shard_map(
        functools.partial(on_device, mesh.shape["wide"], mesh.shape["col"]),
        mesh=mesh,
        in_specs=(P("wide", "col"), P("wide", "col")),
        out_specs=P(("wide", "col"), None),
        check_vma=False,
    )
```

```python
import functools

import jax
import jax.numpy as jnp
from jax import lax
from jax.experimental import pallas as pl
from jax.experimental.pallas import tpu as pltpu
from jax.sharding import PartitionSpec as P

MESH = pl.DeviceIdType.MESH
CORES = 2
PIECES = 2


def halves(x):
    high = x.astype(jnp.bfloat16)
    low = (x - high.astype(jnp.float32)).astype(jnp.bfloat16)
    return high, low


def dot(x, y):
    return lax.dot_general(x, y, (((1,), (1,)), ((), ())), preferred_element_type=jnp.float32)


def kernel(wide, cols, a_ref, b_ref, o_ref, panel, a_high, a_low, part, landed,
           guest, guest_high, guest_low, outbox, inbox,
           send_line, send_pair, recv_panel, send_sum, recv_sum,
           send_guest, recv_guest, send_back, recv_back):
    w = lax.axis_index("wide")
    c = lax.axis_index("col")
    line = wide // CORES
    g = w // CORES
    core = w % CORES
    sibling = g * CORES + 1 - core
    rows = b_ref.shape[0] // PIECES
    share = o_ref.shape[0]
    slots = wide * PIECES
    extra = CORES * PIECES
    far = line - 2
    left_end, right_end = g == 0, g == line - 1
    helps_left, helps_right = g == 1, g == far
    is_end = left_end | right_end
    helps = helps_left | helps_right
    partner = jnp.where(left_end | helps_right, w + CORES, w - CORES)
    first = jnp.where(right_end, extra, 0)
    last = jnp.where(left_end, slots - extra, slots)
    missing = jnp.where(left_end, slots - extra, 0)

    barrier = pltpu.get_barrier_semaphore()

    def greet(wide_index, col_index):
        pl.semaphore_signal(barrier, inc=1, device_id={"wide": wide_index, "col": col_index}, device_id_type=MESH)

    has_left = g > 0
    has_right = g < line - 1
    pl.when(has_left)(lambda: greet(w - CORES, c))
    pl.when(has_right)(lambda: greet(w + CORES, c))
    greet(sibling, c)

    @pl.loop(1, cols)
    def _(j):
        greet(w, (c + j) % cols)

    pl.semaphore_wait(barrier, cols + has_left.astype(jnp.int32) + has_right.astype(jnp.int32))

    def push(src, slot, sem, target):
        return pltpu.make_async_remote_copy(
            src_ref=src, dst_ref=panel.at[slot], send_sem=sem, recv_sem=recv_panel.at[slot],
            device_id={"wide": target, "col": c}, device_id_type=MESH)

    def own(h):
        return b_ref.at[pl.ds(h * rows, rows)]

    def arrive(slot):
        pltpu.make_async_copy(panel.at[slot], panel.at[slot], recv_panel.at[slot]).wait()

    def lend():
        return pltpu.make_async_remote_copy(
            src_ref=a_ref, dst_ref=guest, send_sem=send_guest, recv_sem=recv_guest,
            device_id={"wide": partner, "col": c}, device_id_type=MESH)

    def give_back(i):
        return pltpu.make_async_remote_copy(
            src_ref=outbox.at[i], dst_ref=inbox.at[i], send_sem=send_back.at[i], recv_sem=recv_back.at[i],
            device_id={"wide": partner, "col": c}, device_id_type=MESH)

    def contract(block, slot):
        contract_rows(a_high, a_low, block, slot)

    def contract_guest(slot):
        contract_rows(guest_high, guest_low, panel[slot], slots + slot % extra)

    def contract_rows(rows_high, rows_low, block, slot):
        high, low = halves(block)
        product = dot(rows_high[...], high) + (dot(rows_high[...], low) + dot(rows_low[...], high))
        for k in range(cols):
            part[slot, k] = product[k * share:(k + 1) * share]

        @pl.loop(1, cols)
        def _(j):
            peer = (c + j) % cols
            pltpu.make_async_remote_copy(
                src_ref=part.at[slot, peer], dst_ref=landed.at[slot, cols - 1 - j],
                send_sem=send_sum.at[slot], recv_sem=recv_sum.at[slot],
                device_id={"wide": w, "col": peer}, device_id_type=MESH).start()

    for h in range(PIECES):
        slot = w * PIECES + h
        pl.when(has_right)(lambda: push(own(h), slot, send_line.at[slot], w + CORES).start())
        pl.when(has_left)(lambda: push(own(h), slot, send_line.at[wide * PIECES + h], w - CORES).start())
        push(own(h), slot, send_pair.at[slot], sibling).start()

    high, low = halves(a_ref[...])
    a_high[...] = high
    a_low[...] = low
    for h in range(PIECES):
        contract(b_ref[h * rows:(h + 1) * rows], w * PIECES + h)
    for h in range(PIECES):
        slot = sibling * PIECES + h
        arrive(slot)
        contract(panel[slot], slot)

    @pl.loop(1, line - 1)
    def _(d):
        @pl.loop(0, PIECES)
        def _(h):
            left_slot = (w - d * CORES) * PIECES + h
            right_slot = (w + d * CORES) * PIECES + h
            pair_left = (sibling - d * CORES) * PIECES + h
            pair_right = (sibling + d * CORES) * PIECES + h
            pl.when(is_end & (d == 2) & (h == 0))(lambda: lend().start())

            @pl.when(g - d >= 0)
            def _():
                arrive(left_slot)
                pl.when(has_right & (d < far))(lambda: push(panel.at[left_slot], left_slot, send_line.at[left_slot], w + CORES).start())
                push(panel.at[left_slot], left_slot, send_pair.at[left_slot], sibling).start()

            @pl.when(g + d < line)
            def _():
                arrive(right_slot)
                pl.when(has_left & (d < far))(lambda: push(panel.at[right_slot], right_slot, send_line.at[right_slot], w - CORES).start())
                push(panel.at[right_slot], right_slot, send_pair.at[right_slot], sibling).start()

            @pl.when(helps & (d == far) & (h == 0))
            def _():
                pltpu.make_async_copy(guest, guest, recv_guest).wait()
                high, low = halves(guest[...])
                guest_high[...] = high
                guest_low[...] = low

            pl.when(helps & (d == far))(lambda: contract_guest(jnp.where(helps_left, right_slot, left_slot)))

            @pl.when(g - d >= 0)
            def _():
                contract(panel[left_slot], left_slot)

            @pl.when(g + d < line)
            def _():
                contract(panel[right_slot], right_slot)

            @pl.when(g - d >= 0)
            def _():
                arrive(pair_left)
                contract(panel[pair_left], pair_left)

            @pl.when(g + d < line)
            def _():
                arrive(pair_right)
                contract(panel[pair_right], pair_right)

            pl.when(helps & (d == far))(lambda: contract_guest(jnp.where(helps_left, pair_right, pair_left)))

    def summed(slot):
        pltpu.make_async_copy(landed.at[slot], landed.at[slot], recv_sum.at[slot]).wait()
        total = part[slot, c]
        for k in range(cols - 1):
            total = total + landed[slot, k]
        return total

    def place(slot, block):
        o_ref[:, pl.ds(pl.multiple_of(slot * rows, rows), rows)] = block

    @pl.when(helps)
    def _():
        @pl.loop(0, extra)
        def _(i):
            outbox[i] = summed(slots + i)
            give_back(i).start()

    @pl.loop(0, slots)
    def _(slot):
        pl.when((slot >= first) & (slot < last))(lambda: place(slot, summed(slot)))

    @pl.when(is_end)
    def _():
        @pl.loop(0, extra)
        def _(i):
            pltpu.make_async_copy(inbox.at[i], inbox.at[i], recv_back.at[i]).wait()
            place(missing + i, inbox[i])

    for h in range(PIECES):
        slot = w * PIECES + h
        pl.when(has_right)(lambda: push(own(h), slot, send_line.at[slot], w + CORES).wait_send())
        pl.when(has_left)(lambda: push(own(h), slot, send_line.at[wide * PIECES + h], w - CORES).wait_send())
        push(own(h), slot, send_pair.at[slot], sibling).wait_send()

    @pl.loop(1, line - 1)
    def _(d):
        @pl.loop(0, PIECES)
        def _(h):
            left_slot = (w - d * CORES) * PIECES + h
            right_slot = (w + d * CORES) * PIECES + h

            @pl.when(g - d >= 0)
            def _():
                pl.when(has_right & (d < far))(lambda: push(panel.at[left_slot], left_slot, send_line.at[left_slot], w + CORES).wait_send())
                push(panel.at[left_slot], left_slot, send_pair.at[left_slot], sibling).wait_send()

            @pl.when(g + d < line)
            def _():
                pl.when(has_left & (d < far))(lambda: push(panel.at[right_slot], right_slot, send_line.at[right_slot], w - CORES).wait_send())
                push(panel.at[right_slot], right_slot, send_pair.at[right_slot], sibling).wait_send()

    def sent(slot):
        pltpu.make_async_copy(landed.at[slot], landed.at[slot], send_sum.at[slot]).wait()

    @pl.loop(0, slots)
    def _(slot):
        pl.when((slot >= first) & (slot < last))(lambda: sent(slot))

    @pl.when(helps)
    def _():
        @pl.loop(0, extra)
        def _(i):
            sent(slots + i)
            give_back(i).wait_send()

    pl.when(is_end)(lambda: lend().wait_send())


def on_device(wide, cols, amplitudes, integrals):
    rows_a, depth = amplitudes.shape
    rows_b = integrals.shape[0]
    share = rows_a // cols
    slots = wide * PIECES
    extra = CORES * PIECES
    rows = rows_b // PIECES
    vmem = pl.BlockSpec(memory_space=pltpu.VMEM)
    return pl.pallas_call(
        functools.partial(kernel, wide, cols),
        out_shape=jax.ShapeDtypeStruct((share, wide * rows_b), jnp.float32),
        in_specs=[vmem, vmem],
        out_specs=vmem,
        scratch_shapes=[
            pltpu.VMEM((slots, rows, depth), jnp.float32),
            pltpu.VMEM((rows_a, depth), jnp.bfloat16),
            pltpu.VMEM((rows_a, depth), jnp.bfloat16),
            pltpu.VMEM((slots + extra, cols, share, rows), jnp.float32),
            pltpu.VMEM((slots + extra, cols - 1, share, rows), jnp.float32),
            pltpu.VMEM((rows_a, depth), jnp.float32),
            pltpu.VMEM((rows_a, depth), jnp.bfloat16),
            pltpu.VMEM((rows_a, depth), jnp.bfloat16),
            pltpu.VMEM((extra, share, rows), jnp.float32),
            pltpu.VMEM((extra, share, rows), jnp.float32),
            pltpu.SemaphoreType.DMA((slots + PIECES,)),
            pltpu.SemaphoreType.DMA((slots,)),
            pltpu.SemaphoreType.DMA((slots,)),
            pltpu.SemaphoreType.DMA((slots + extra,)),
            pltpu.SemaphoreType.DMA((slots + extra,)),
            pltpu.SemaphoreType.DMA,
            pltpu.SemaphoreType.DMA,
            pltpu.SemaphoreType.DMA((extra,)),
            pltpu.SemaphoreType.DMA((extra,)),
        ],
        compiler_params=pltpu.CompilerParams(
            collective_id=0, has_side_effects=True, vmem_limit_bytes=56 * 1024 * 1024),
    )(amplitudes, integrals)


def solution(mesh):
    return jax.shard_map(
        functools.partial(on_device, mesh.shape["wide"], mesh.shape["col"]),
        mesh=mesh,
        in_specs=(P("wide", "col"), P("wide", "col")),
        out_specs=P(("wide", "col"), None),
        check_vma=False,
    )
```

```python
import functools

import jax
import jax.numpy as jnp
from jax import lax
from jax.experimental import pallas as pl
from jax.experimental.pallas import tpu as pltpu
from jax.sharding import PartitionSpec as P

MESH = pl.DeviceIdType.MESH
CORES = 2
PIECES = 2


def inner_factor(cols):
    return max(k for k in range(1, cols + 1) if cols % k == 0 and k * k <= cols)


def halves(x):
    high = x.astype(jnp.bfloat16)
    low = (x - high.astype(jnp.float32)).astype(jnp.bfloat16)
    return high, low


def dot(x, y):
    return lax.dot_general(x, y, (((1,), (1,)), ((), ())), preferred_element_type=jnp.float32)


def kernel(wide, cols, a_ref, b_ref, o_ref, panel, a_high, a_low, part, landed, mid, landed_mid,
           guest, guest_high, guest_low, outbox, inbox,
           send_line, send_pair, recv_panel, send_sum, recv_sum, send_mid, recv_mid,
           send_guest, recv_guest, send_back, recv_back):
    w = lax.axis_index("wide")
    c = lax.axis_index("col")
    line = wide // CORES
    g = w // CORES
    core = w % CORES
    sibling = g * CORES + 1 - core
    rows = b_ref.shape[0] // PIECES
    share = o_ref.shape[0]
    slots = wide * PIECES
    extra = CORES * PIECES
    far = line - 2
    left_end, right_end = g == 0, g == line - 1
    helps_left, helps_right = g == 1, g == far
    is_end = left_end | right_end
    helps = helps_left | helps_right
    partner = jnp.where(left_end | helps_right, w + CORES, w - CORES)
    first = jnp.where(right_end, extra, 0)
    last = jnp.where(left_end, slots - extra, slots)
    missing = jnp.where(left_end, slots - extra, 0)
    inner = inner_factor(cols)
    outer = cols // inner

    def route(h):
        if h % 2 == 0:
            return outer, inner, c // inner, c % inner, lambda f, s: f * inner + s
        return inner, outer, c % inner, c // inner, lambda f, s: s * inner + f

    barrier = pltpu.get_barrier_semaphore()

    def greet(wide_index, col_index):
        pl.semaphore_signal(barrier, inc=1, device_id={"wide": wide_index, "col": col_index}, device_id_type=MESH)

    has_left = g > 0
    has_right = g < line - 1
    pl.when(has_left)(lambda: greet(w - CORES, c))
    pl.when(has_right)(lambda: greet(w + CORES, c))
    greet(sibling, c)

    @pl.loop(1, cols)
    def _(j):
        greet(w, (c + j) % cols)

    pl.semaphore_wait(barrier, cols + has_left.astype(jnp.int32) + has_right.astype(jnp.int32))

    def push(src, slot, sem, target):
        return pltpu.make_async_remote_copy(
            src_ref=src, dst_ref=panel.at[slot], send_sem=sem, recv_sem=recv_panel.at[slot],
            device_id={"wide": target, "col": c}, device_id_type=MESH)

    def own(h):
        return b_ref.at[pl.ds(h * rows, rows)]

    def arrive(slot):
        pltpu.make_async_copy(panel.at[slot], panel.at[slot], recv_panel.at[slot]).wait()

    def lend():
        return pltpu.make_async_remote_copy(
            src_ref=a_ref, dst_ref=guest, send_sem=send_guest, recv_sem=recv_guest,
            device_id={"wide": partner, "col": c}, device_id_type=MESH)

    def give_back(i):
        return pltpu.make_async_remote_copy(
            src_ref=outbox.at[i], dst_ref=inbox.at[i], send_sem=send_back.at[i], recv_sem=recv_back.at[i],
            device_id={"wide": partner, "col": c}, device_id_type=MESH)

    def contract(block, slot, h):
        contract_rows(a_high, a_low, block, slot, h)

    def contract_guest(slot, h):
        contract_rows(guest_high, guest_low, panel[slot], slots + slot % extra, h)

    def contract_rows(rows_high, rows_low, block, slot, h):
        high, low = halves(block)
        product = dot(rows_high[...], high) + (dot(rows_high[...], low) + dot(rows_low[...], high))
        nf, ns, f, s, col_of = route(h)
        for i in range(nf):
            for k in range(ns):
                row = col_of(i, k) * share
                part[slot, i * ns + k] = product[row:row + share]

        for j in range(1, nf):
            peer = (f + j) % nf
            pltpu.make_async_remote_copy(
                src_ref=part.at[slot, pl.ds(peer * ns, ns)],
                dst_ref=landed.at[slot, pl.ds((nf - 1 - j) * ns, ns)],
                send_sem=send_sum.at[slot], recv_sem=recv_sum.at[slot],
                device_id={"wide": w, "col": col_of(peer, s)}, device_id_type=MESH).start()

    def take(ref, slot, count, sem):
        view = ref.at[slot, pl.ds(0, count)]
        pltpu.make_async_copy(view, view, sem.at[slot]).wait()

    def relay(slot, h):
        nf, ns, f, s, col_of = route(h)
        take(landed, slot, (nf - 1) * ns, recv_sum)
        total = part[slot, pl.ds(f * ns, ns)]
        for i in range(nf - 1):
            total = total + landed[slot, i * ns:(i + 1) * ns]
        mid[slot, 0:ns] = total
        for j in range(1, ns):
            peer = (s + j) % ns
            pltpu.make_async_remote_copy(
                src_ref=mid.at[slot, peer], dst_ref=landed_mid.at[slot, ns - 1 - j],
                send_sem=send_mid.at[slot], recv_sem=recv_mid.at[slot],
                device_id={"wide": w, "col": col_of(f, peer)}, device_id_type=MESH).start()

    for h in range(PIECES):
        slot = w * PIECES + h
        pl.when(has_right)(lambda: push(own(h), slot, send_line.at[slot], w + CORES).start())
        pl.when(has_left)(lambda: push(own(h), slot, send_line.at[wide * PIECES + h], w - CORES).start())
        push(own(h), slot, send_pair.at[slot], sibling).start()

    high, low = halves(a_ref[...])
    a_high[...] = high
    a_low[...] = low
    for h in range(PIECES):
        contract(b_ref[h * rows:(h + 1) * rows], w * PIECES + h, h)
    for h in range(PIECES):
        slot = sibling * PIECES + h
        arrive(slot)
        contract(panel[slot], slot, h)

    def relay_step(d, h):
        @pl.when(g - d >= 0)
        def _():
            relay((w - d * CORES) * PIECES + h, h)
            relay((sibling - d * CORES) * PIECES + h, h)

        @pl.when(g + d < line)
        def _():
            relay((w + d * CORES) * PIECES + h, h)
            relay((sibling + d * CORES) * PIECES + h, h)

    @pl.loop(1, line - 1)
    def _(d):
        for h in range(PIECES):
            left_slot = (w - d * CORES) * PIECES + h
            right_slot = (w + d * CORES) * PIECES + h
            pair_left = (sibling - d * CORES) * PIECES + h
            pair_right = (sibling + d * CORES) * PIECES + h

            @pl.when(g - d >= 0)
            def _():
                arrive(left_slot)
                pl.when(has_right & (d < far))(lambda: push(panel.at[left_slot], left_slot, send_line.at[left_slot], w + CORES).start())
                push(panel.at[left_slot], left_slot, send_pair.at[left_slot], sibling).start()

            @pl.when(g + d < line)
            def _():
                arrive(right_slot)
                pl.when(has_left & (d < far))(lambda: push(panel.at[right_slot], right_slot, send_line.at[right_slot], w - CORES).start())
                push(panel.at[right_slot], right_slot, send_pair.at[right_slot], sibling).start()

            pl.when(is_end & (d == (1 if h == PIECES - 1 else 0)))(lambda: lend().start())

            @pl.when(g - d >= 0)
            def _():
                contract(panel[left_slot], left_slot, h)

            @pl.when(g + d < line)
            def _():
                contract(panel[right_slot], right_slot, h)

            @pl.when(g - d >= 0)
            def _():
                arrive(pair_left)
                contract(panel[pair_left], pair_left, h)

            @pl.when(g + d < line)
            def _():
                arrive(pair_right)
                contract(panel[pair_right], pair_right, h)

            if h > 0:
                relay_step(d, h - 1)
            else:
                @pl.when(d == 1)
                def _():
                    for p in range(PIECES):
                        relay(w * PIECES + p, p)
                        relay(sibling * PIECES + p, p)

                pl.when(d > 1)(lambda: relay_step(d - 1, PIECES - 1))

    relay_step(line - 2, PIECES - 1)

    def summed(slot, h):
        nf, ns, f, s, col_of = route(h)
        take(landed_mid, slot, ns - 1, recv_mid)
        total = mid[slot, s]
        for k in range(ns - 1):
            total = total + landed_mid[slot, k]
        return total

    def place(slot, block):
        o_ref[:, pl.ds(pl.multiple_of(slot * rows, rows), rows)] = block

    @pl.when(helps)
    def _():
        pltpu.make_async_copy(guest, guest, recv_guest).wait()
        high, low = halves(guest[...])
        guest_high[...] = high
        guest_low[...] = low
        start = jnp.where(helps_left, slots - extra, 0)

        for i in range(extra):
            contract_guest(start + i, i % PIECES)
        for i in range(extra):
            relay(slots + i, i % PIECES)
        for i in range(extra):
            outbox[i] = summed(slots + i, i % PIECES)
            give_back(i).start()

    @pl.loop(0, wide)
    def _(q):
        for h in range(PIECES):
            slot = q * PIECES + h
            pl.when((slot >= first) & (slot < last))(lambda: place(slot, summed(slot, h)))

    @pl.when(is_end)
    def _():
        @pl.loop(0, extra)
        def _(i):
            pltpu.make_async_copy(inbox.at[i], inbox.at[i], recv_back.at[i]).wait()
            place(missing + i, inbox[i])

    for h in range(PIECES):
        slot = w * PIECES + h
        pl.when(has_right)(lambda: push(own(h), slot, send_line.at[slot], w + CORES).wait_send())
        pl.when(has_left)(lambda: push(own(h), slot, send_line.at[wide * PIECES + h], w - CORES).wait_send())
        push(own(h), slot, send_pair.at[slot], sibling).wait_send()

    @pl.loop(1, line - 1)
    def _(d):
        @pl.loop(0, PIECES)
        def _(h):
            left_slot = (w - d * CORES) * PIECES + h
            right_slot = (w + d * CORES) * PIECES + h

            @pl.when(g - d >= 0)
            def _():
                pl.when(has_right & (d < far))(lambda: push(panel.at[left_slot], left_slot, send_line.at[left_slot], w + CORES).wait_send())
                push(panel.at[left_slot], left_slot, send_pair.at[left_slot], sibling).wait_send()

            @pl.when(g + d < line)
            def _():
                pl.when(has_left & (d < far))(lambda: push(panel.at[right_slot], right_slot, send_line.at[right_slot], w - CORES).wait_send())
                push(panel.at[right_slot], right_slot, send_pair.at[right_slot], sibling).wait_send()

    def sent(slot, h):
        nf, ns, f, s, col_of = route(h)
        take(landed, slot, (nf - 1) * ns, send_sum)
        take(landed_mid, slot, ns - 1, send_mid)

    @pl.loop(0, wide)
    def _(q):
        for h in range(PIECES):
            slot = q * PIECES + h
            pl.when((slot >= first) & (slot < last))(lambda: sent(slot, h))

    @pl.when(helps)
    def _():
        for i in range(extra):
            sent(slots + i, i % PIECES)
            give_back(i).wait_send()

    pl.when(is_end)(lambda: lend().wait_send())


def on_device(wide, cols, amplitudes, integrals):
    rows_a, depth = amplitudes.shape
    rows_b = integrals.shape[0]
    share = rows_a // cols
    slots = wide * PIECES
    extra = CORES * PIECES
    rows = rows_b // PIECES
    vmem = pl.BlockSpec(memory_space=pltpu.VMEM)
    return pl.pallas_call(
        functools.partial(kernel, wide, cols),
        out_shape=jax.ShapeDtypeStruct((share, wide * rows_b), jnp.float32),
        in_specs=[vmem, vmem],
        out_specs=vmem,
        scratch_shapes=[
            pltpu.VMEM((slots, rows, depth), jnp.float32),
            pltpu.VMEM((rows_a, depth), jnp.bfloat16),
            pltpu.VMEM((rows_a, depth), jnp.bfloat16),
            pltpu.VMEM((slots + extra, cols, share, rows), jnp.float32),
            pltpu.VMEM((slots + extra, cols - 1, share, rows), jnp.float32),
            pltpu.VMEM((slots + extra, cols // inner_factor(cols), share, rows), jnp.float32),
            pltpu.VMEM((slots + extra, cols // inner_factor(cols) - 1, share, rows), jnp.float32),
            pltpu.VMEM((rows_a, depth), jnp.float32),
            pltpu.VMEM((rows_a, depth), jnp.bfloat16),
            pltpu.VMEM((rows_a, depth), jnp.bfloat16),
            pltpu.VMEM((extra, share, rows), jnp.float32),
            pltpu.VMEM((extra, share, rows), jnp.float32),
            pltpu.SemaphoreType.DMA((slots + PIECES,)),
            pltpu.SemaphoreType.DMA((slots,)),
            pltpu.SemaphoreType.DMA((slots,)),
            pltpu.SemaphoreType.DMA((slots + extra,)),
            pltpu.SemaphoreType.DMA((slots + extra,)),
            pltpu.SemaphoreType.DMA((slots + extra,)),
            pltpu.SemaphoreType.DMA((slots + extra,)),
            pltpu.SemaphoreType.DMA,
            pltpu.SemaphoreType.DMA,
            pltpu.SemaphoreType.DMA((extra,)),
            pltpu.SemaphoreType.DMA((extra,)),
        ],
        compiler_params=pltpu.CompilerParams(
            collective_id=0, has_side_effects=True, vmem_limit_bytes=56 * 1024 * 1024),
    )(amplitudes, integrals)


def solution(mesh):
    return jax.shard_map(
        functools.partial(on_device, mesh.shape["wide"], mesh.shape["col"]),
        mesh=mesh,
        in_specs=(P("wide", "col"), P("wide", "col")),
        out_specs=P(("wide", "col"), None),
        check_vma=False,
    )
```

```python
import functools

import jax
import jax.numpy as jnp
from jax import lax
from jax.experimental import pallas as pl
from jax.experimental.pallas import tpu as pltpu
from jax.sharding import PartitionSpec as P

MESH = pl.DeviceIdType.MESH
CORES = 2
PIECES = 2
LENT = PIECES - 1


def halves(x):
    high = x.astype(jnp.bfloat16)
    low = (x - high.astype(jnp.float32)).astype(jnp.bfloat16)
    return high, low


def dot(x, y):
    return lax.dot_general(x, y, (((1,), (1,)), ((), ())), preferred_element_type=jnp.float32)


def kernel(wide, cols, a_ref, b_ref, o_ref, panel, a_high, a_low, part, landed,
           guest, guest_high, guest_low, outbox, inbox,
           send_line, send_pair, recv_panel, send_sum, recv_sum,
           send_guest, recv_guest, send_back, recv_back):
    w = lax.axis_index("wide")
    c = lax.axis_index("col")
    line = wide // CORES
    g = w // CORES
    core = w % CORES
    sibling = g * CORES + 1 - core
    rows = b_ref.shape[0] // PIECES
    share = o_ref.shape[0]
    slots = wide * PIECES
    extra = CORES
    far = line - 2
    left_end, right_end = g == 0, g == line - 1
    helps_left, helps_right = g == 1, g == far
    is_end = left_end | right_end
    helps = helps_left | helps_right
    partner = jnp.where(left_end | helps_right, w + CORES, w - CORES)
    chip_slots = CORES * PIECES
    missing = jnp.where(left_end, slots - chip_slots, 0) + LENT

    def kept(slot):
        lacks = (left_end & (slot >= slots - chip_slots)) | (right_end & (slot < chip_slots))
        return ~(lacks & (slot % PIECES == LENT))

    barrier = pltpu.get_barrier_semaphore()

    def greet(wide_index, col_index):
        pl.semaphore_signal(barrier, inc=1, device_id={"wide": wide_index, "col": col_index}, device_id_type=MESH)

    has_left = g > 0
    has_right = g < line - 1
    pl.when(has_left)(lambda: greet(w - CORES, c))
    pl.when(has_right)(lambda: greet(w + CORES, c))
    greet(sibling, c)

    @pl.loop(1, cols)
    def _(j):
        greet(w, (c + j) % cols)

    pl.semaphore_wait(barrier, cols + has_left.astype(jnp.int32) + has_right.astype(jnp.int32))

    def push(src, slot, sem, target):
        return pltpu.make_async_remote_copy(
            src_ref=src, dst_ref=panel.at[slot], send_sem=sem, recv_sem=recv_panel.at[slot],
            device_id={"wide": target, "col": c}, device_id_type=MESH)

    def own(h):
        return b_ref.at[pl.ds(h * rows, rows)]

    def arrive(slot):
        pltpu.make_async_copy(panel.at[slot], panel.at[slot], recv_panel.at[slot]).wait()

    def lend():
        return pltpu.make_async_remote_copy(
            src_ref=a_ref, dst_ref=guest, send_sem=send_guest, recv_sem=recv_guest,
            device_id={"wide": partner, "col": c}, device_id_type=MESH)

    def give_back(i):
        return pltpu.make_async_remote_copy(
            src_ref=outbox.at[i], dst_ref=inbox.at[i], send_sem=send_back.at[i], recv_sem=recv_back.at[i],
            device_id={"wide": partner, "col": c}, device_id_type=MESH)

    def contract(block, slot):
        contract_rows(a_high, a_low, block, slot)

    def contract_guest(slot, i):
        contract_rows(guest_high, guest_low, panel[slot], slots + i)

    def contract_rows(rows_high, rows_low, block, slot):
        high, low = halves(block)
        product = dot(rows_high[...], high) + (dot(rows_high[...], low) + dot(rows_low[...], high))
        for k in range(cols):
            part[slot, k] = product[k * share:(k + 1) * share]

        @pl.loop(1, cols)
        def _(j):
            peer = (c + j) % cols
            pltpu.make_async_remote_copy(
                src_ref=part.at[slot, peer], dst_ref=landed.at[slot, cols - 1 - j],
                send_sem=send_sum.at[slot], recv_sem=recv_sum.at[slot],
                device_id={"wide": w, "col": peer}, device_id_type=MESH).start()

    for h in range(PIECES):
        slot = w * PIECES + h
        pl.when(has_right)(lambda: push(own(h), slot, send_line.at[slot], w + CORES).start())
        pl.when(has_left)(lambda: push(own(h), slot, send_line.at[wide * PIECES + h], w - CORES).start())
        push(own(h), slot, send_pair.at[slot], sibling).start()

    high, low = halves(a_ref[...])
    a_high[...] = high
    a_low[...] = low
    for h in range(PIECES):
        contract(b_ref[h * rows:(h + 1) * rows], w * PIECES + h)
    for h in range(PIECES):
        slot = sibling * PIECES + h
        arrive(slot)
        contract(panel[slot], slot)

    @pl.loop(1, line)
    def _(d):
        @pl.loop(0, PIECES)
        def _(h):
            left_slot = (w - d * CORES) * PIECES + h
            right_slot = (w + d * CORES) * PIECES + h
            pair_left = (sibling - d * CORES) * PIECES + h
            pair_right = (sibling + d * CORES) * PIECES + h

            @pl.when((g - d >= 0) & ((d <= far) | (h < LENT)))
            def _():
                arrive(left_slot)
                pl.when(has_right & ((d < far) | ((d == far) & (h < LENT))))(lambda: push(panel.at[left_slot], left_slot, send_line.at[left_slot], w + CORES).start())
                push(panel.at[left_slot], left_slot, send_pair.at[left_slot], sibling).start()

            @pl.when((g + d < line) & ((d <= far) | (h < LENT)))
            def _():
                arrive(right_slot)
                pl.when(has_left & ((d < far) | ((d == far) & (h < LENT))))(lambda: push(panel.at[right_slot], right_slot, send_line.at[right_slot], w - CORES).start())
                push(panel.at[right_slot], right_slot, send_pair.at[right_slot], sibling).start()

            pl.when(is_end & (d == 1) & (h == PIECES - 1))(lambda: lend().start())

            @pl.when((g - d >= 0) & ((d <= far) | (h < LENT)))
            def _():
                contract(panel[left_slot], left_slot)

            @pl.when((g + d < line) & ((d <= far) | (h < LENT)))
            def _():
                contract(panel[right_slot], right_slot)

            @pl.when((g - d >= 0) & ((d <= far) | (h < LENT)))
            def _():
                arrive(pair_left)
                contract(panel[pair_left], pair_left)

            @pl.when((g + d < line) & ((d <= far) | (h < LENT)))
            def _():
                arrive(pair_right)
                contract(panel[pair_right], pair_right)

    def summed(slot):
        pltpu.make_async_copy(landed.at[slot], landed.at[slot], recv_sum.at[slot]).wait()
        total = part[slot, c]
        for k in range(cols - 1):
            total = total + landed[slot, k]
        return total

    def place(slot, block):
        o_ref[:, pl.ds(pl.multiple_of(slot * rows, rows), rows)] = block

    @pl.when(helps)
    def _():
        pltpu.make_async_copy(guest, guest, recv_guest).wait()
        high, low = halves(guest[...])
        guest_high[...] = high
        guest_low[...] = low
        start = jnp.where(helps_left, slots - chip_slots, 0) + LENT

        @pl.loop(0, extra)
        def _(i):
            contract_guest(start + i * PIECES, i)

        @pl.loop(0, extra)
        def _(i):
            outbox[i] = summed(slots + i)
            give_back(i).start()

    @pl.loop(0, slots)
    def _(slot):
        pl.when(kept(slot))(lambda: place(slot, summed(slot)))

    @pl.when(is_end)
    def _():
        @pl.loop(0, extra)
        def _(i):
            pltpu.make_async_copy(inbox.at[i], inbox.at[i], recv_back.at[i]).wait()
            place(missing + i * PIECES, inbox[i])

    for h in range(PIECES):
        slot = w * PIECES + h
        pl.when(has_right)(lambda: push(own(h), slot, send_line.at[slot], w + CORES).wait_send())
        pl.when(has_left)(lambda: push(own(h), slot, send_line.at[wide * PIECES + h], w - CORES).wait_send())
        push(own(h), slot, send_pair.at[slot], sibling).wait_send()

    @pl.loop(1, line)
    def _(d):
        @pl.loop(0, PIECES)
        def _(h):
            left_slot = (w - d * CORES) * PIECES + h
            right_slot = (w + d * CORES) * PIECES + h

            @pl.when((g - d >= 0) & ((d <= far) | (h < LENT)))
            def _():
                pl.when(has_right & ((d < far) | ((d == far) & (h < LENT))))(lambda: push(panel.at[left_slot], left_slot, send_line.at[left_slot], w + CORES).wait_send())
                push(panel.at[left_slot], left_slot, send_pair.at[left_slot], sibling).wait_send()

            @pl.when((g + d < line) & ((d <= far) | (h < LENT)))
            def _():
                pl.when(has_left & ((d < far) | ((d == far) & (h < LENT))))(lambda: push(panel.at[right_slot], right_slot, send_line.at[right_slot], w - CORES).wait_send())
                push(panel.at[right_slot], right_slot, send_pair.at[right_slot], sibling).wait_send()

    def sent(slot):
        pltpu.make_async_copy(landed.at[slot], landed.at[slot], send_sum.at[slot]).wait()

    @pl.loop(0, slots)
    def _(slot):
        pl.when(kept(slot))(lambda: sent(slot))

    @pl.when(helps)
    def _():
        @pl.loop(0, extra)
        def _(i):
            sent(slots + i)
            give_back(i).wait_send()

    pl.when(is_end)(lambda: lend().wait_send())


def on_device(wide, cols, amplitudes, integrals):
    rows_a, depth = amplitudes.shape
    rows_b = integrals.shape[0]
    share = rows_a // cols
    slots = wide * PIECES
    extra = CORES
    rows = rows_b // PIECES
    vmem = pl.BlockSpec(memory_space=pltpu.VMEM)
    return pl.pallas_call(
        functools.partial(kernel, wide, cols),
        out_shape=jax.ShapeDtypeStruct((share, wide * rows_b), jnp.float32),
        in_specs=[vmem, vmem],
        out_specs=vmem,
        scratch_shapes=[
            pltpu.VMEM((slots, rows, depth), jnp.float32),
            pltpu.VMEM((rows_a, depth), jnp.bfloat16),
            pltpu.VMEM((rows_a, depth), jnp.bfloat16),
            pltpu.VMEM((slots + extra, cols, share, rows), jnp.float32),
            pltpu.VMEM((slots + extra, cols - 1, share, rows), jnp.float32),
            pltpu.VMEM((rows_a, depth), jnp.float32),
            pltpu.VMEM((rows_a, depth), jnp.bfloat16),
            pltpu.VMEM((rows_a, depth), jnp.bfloat16),
            pltpu.VMEM((extra, share, rows), jnp.float32),
            pltpu.VMEM((extra, share, rows), jnp.float32),
            pltpu.SemaphoreType.DMA((slots + PIECES,)),
            pltpu.SemaphoreType.DMA((slots,)),
            pltpu.SemaphoreType.DMA((slots,)),
            pltpu.SemaphoreType.DMA((slots + extra,)),
            pltpu.SemaphoreType.DMA((slots + extra,)),
            pltpu.SemaphoreType.DMA,
            pltpu.SemaphoreType.DMA,
            pltpu.SemaphoreType.DMA((extra,)),
            pltpu.SemaphoreType.DMA((extra,)),
        ],
        compiler_params=pltpu.CompilerParams(
            collective_id=0, has_side_effects=True, vmem_limit_bytes=56 * 1024 * 1024),
    )(amplitudes, integrals)


def solution(mesh):
    return jax.shard_map(
        functools.partial(on_device, mesh.shape["wide"], mesh.shape["col"]),
        mesh=mesh,
        in_specs=(P("wide", "col"), P("wide", "col")),
        out_specs=P(("wide", "col"), None),
        check_vma=False,
    )
```

```python
import functools

import jax
import jax.numpy as jnp
from jax import lax
from jax.experimental import pallas as pl
from jax.experimental.pallas import tpu as pltpu
from jax.sharding import PartitionSpec as P

MESH = pl.DeviceIdType.MESH
CORES = 2
PIECES = 2
LENT = PIECES - 1


def halves(x):
    high = x.astype(jnp.bfloat16)
    low = (x - high.astype(jnp.float32)).astype(jnp.bfloat16)
    return high, low


def dot(x, y):
    return lax.dot_general(x, y, (((1,), (1,)), ((), ())), preferred_element_type=jnp.float32)


def kernel(wide, cols, a_hbm, b_hbm, o_ref, a_ref, b_ref, load_sem, panel, a_high, a_low, part, landed,
           guest, guest_high, guest_low, outbox, inbox,
           send_line, send_pair, recv_panel, send_sum, recv_sum,
           send_guest, recv_guest, send_back, recv_back):
    w = lax.axis_index("wide")
    c = lax.axis_index("col")
    line = wide // CORES
    g = w // CORES
    core = w % CORES
    sibling = g * CORES + 1 - core
    rows = b_ref.shape[0] // PIECES
    share = o_ref.shape[0]
    slots = wide * PIECES
    extra = CORES
    far = line - 2
    left_end, right_end = g == 0, g == line - 1
    helps_left, helps_right = g == 1, g == far
    is_end = left_end | right_end
    helps = helps_left | helps_right
    partner = jnp.where(left_end | helps_right, w + CORES, w - CORES)
    chip_slots = CORES * PIECES
    missing = jnp.where(left_end, slots - chip_slots, 0) + LENT

    def kept(slot):
        lacks = (left_end & (slot >= slots - chip_slots)) | (right_end & (slot < chip_slots))
        return ~(lacks & (slot % PIECES == LENT))

    load_a = pltpu.make_async_copy(a_hbm, a_ref, load_sem.at[0])
    load_b = pltpu.make_async_copy(b_hbm, b_ref, load_sem.at[1])
    load_b.start()
    load_a.start()
    barrier = pltpu.get_barrier_semaphore()

    def greet(wide_index, col_index):
        pl.semaphore_signal(barrier, inc=1, device_id={"wide": wide_index, "col": col_index}, device_id_type=MESH)

    has_left = g > 0
    has_right = g < line - 1
    pl.when(has_left)(lambda: greet(w - CORES, c))
    pl.when(has_right)(lambda: greet(w + CORES, c))
    greet(sibling, c)

    @pl.loop(1, cols)
    def _(j):
        greet(w, (c + j) % cols)

    pl.semaphore_wait(barrier, cols + has_left.astype(jnp.int32) + has_right.astype(jnp.int32))

    load_b.wait()

    def push(src, slot, sem, target):
        return pltpu.make_async_remote_copy(
            src_ref=src, dst_ref=panel.at[slot], send_sem=sem, recv_sem=recv_panel.at[slot],
            device_id={"wide": target, "col": c}, device_id_type=MESH)

    def own(h):
        return b_ref.at[pl.ds(h * rows, rows)]

    def arrive(slot):
        pltpu.make_async_copy(panel.at[slot], panel.at[slot], recv_panel.at[slot]).wait()

    def lend():
        return pltpu.make_async_remote_copy(
            src_ref=a_ref, dst_ref=guest, send_sem=send_guest, recv_sem=recv_guest,
            device_id={"wide": partner, "col": c}, device_id_type=MESH)

    def give_back(i):
        return pltpu.make_async_remote_copy(
            src_ref=outbox.at[i], dst_ref=inbox.at[i], send_sem=send_back.at[i], recv_sem=recv_back.at[i],
            device_id={"wide": partner, "col": c}, device_id_type=MESH)

    def contract(block, slot):
        contract_rows(a_high, a_low, block, slot)

    def contract_guest(slot, i):
        contract_rows(guest_high, guest_low, panel[slot], slots + i)

    def contract_rows(rows_high, rows_low, block, slot):
        high, low = halves(block)
        product = dot(rows_high[...], high) + (dot(rows_high[...], low) + dot(rows_low[...], high))
        for k in range(cols):
            part[slot, k] = product[k * share:(k + 1) * share]

        @pl.loop(1, cols)
        def _(j):
            peer = (c + j) % cols
            pltpu.make_async_remote_copy(
                src_ref=part.at[slot, peer], dst_ref=landed.at[slot, cols - 1 - j],
                send_sem=send_sum.at[slot], recv_sem=recv_sum.at[slot],
                device_id={"wide": w, "col": peer}, device_id_type=MESH).start()

    for h in range(PIECES):
        slot = w * PIECES + h
        pl.when(has_right)(lambda: push(own(h), slot, send_line.at[slot], w + CORES).start())
        pl.when(has_left)(lambda: push(own(h), slot, send_line.at[wide * PIECES + h], w - CORES).start())
        push(own(h), slot, send_pair.at[slot], sibling).start()

    load_a.wait()
    high, low = halves(a_ref[...])
    a_high[...] = high
    a_low[...] = low
    for h in range(PIECES):
        contract(b_ref[h * rows:(h + 1) * rows], w * PIECES + h)
    for h in range(PIECES):
        slot = sibling * PIECES + h
        arrive(slot)
        contract(panel[slot], slot)

    @pl.loop(1, line)
    def _(d):
        @pl.loop(0, PIECES)
        def _(h):
            left_slot = (w - d * CORES) * PIECES + h
            right_slot = (w + d * CORES) * PIECES + h
            pair_left = (sibling - d * CORES) * PIECES + h
            pair_right = (sibling + d * CORES) * PIECES + h

            @pl.when((g - d >= 0) & ((d <= far) | (h < LENT)))
            def _():
                arrive(left_slot)
                pl.when(has_right & ((d < far) | ((d == far) & (h < LENT))))(lambda: push(panel.at[left_slot], left_slot, send_line.at[left_slot], w + CORES).start())
                push(panel.at[left_slot], left_slot, send_pair.at[left_slot], sibling).start()

            @pl.when((g + d < line) & ((d <= far) | (h < LENT)))
            def _():
                arrive(right_slot)
                pl.when(has_left & ((d < far) | ((d == far) & (h < LENT))))(lambda: push(panel.at[right_slot], right_slot, send_line.at[right_slot], w - CORES).start())
                push(panel.at[right_slot], right_slot, send_pair.at[right_slot], sibling).start()

            pl.when(is_end & (d == 1) & (h == PIECES - 1))(lambda: lend().start())

            @pl.when((g - d >= 0) & ((d <= far) | (h < LENT)))
            def _():
                contract(panel[left_slot], left_slot)

            @pl.when((g + d < line) & ((d <= far) | (h < LENT)))
            def _():
                contract(panel[right_slot], right_slot)

            @pl.when((g - d >= 0) & ((d <= far) | (h < LENT)))
            def _():
                arrive(pair_left)
                contract(panel[pair_left], pair_left)

            @pl.when((g + d < line) & ((d <= far) | (h < LENT)))
            def _():
                arrive(pair_right)
                contract(panel[pair_right], pair_right)

    def summed(slot):
        pltpu.make_async_copy(landed.at[slot], landed.at[slot], recv_sum.at[slot]).wait()
        total = part[slot, c]
        for k in range(cols - 1):
            total = total + landed[slot, k]
        return total

    def place(slot, block):
        o_ref[:, pl.ds(pl.multiple_of(slot * rows, rows), rows)] = block

    @pl.when(helps)
    def _():
        pltpu.make_async_copy(guest, guest, recv_guest).wait()
        high, low = halves(guest[...])
        guest_high[...] = high
        guest_low[...] = low
        start = jnp.where(helps_left, slots - chip_slots, 0) + LENT

        @pl.loop(0, extra)
        def _(i):
            contract_guest(start + i * PIECES, i)

        @pl.loop(0, extra)
        def _(i):
            outbox[i] = summed(slots + i)
            give_back(i).start()

    @pl.loop(0, slots)
    def _(slot):
        pl.when(kept(slot))(lambda: place(slot, summed(slot)))

    @pl.when(is_end)
    def _():
        @pl.loop(0, extra)
        def _(i):
            pltpu.make_async_copy(inbox.at[i], inbox.at[i], recv_back.at[i]).wait()
            place(missing + i * PIECES, inbox[i])

    for h in range(PIECES):
        slot = w * PIECES + h
        pl.when(has_right)(lambda: push(own(h), slot, send_line.at[slot], w + CORES).wait_send())
        pl.when(has_left)(lambda: push(own(h), slot, send_line.at[wide * PIECES + h], w - CORES).wait_send())
        push(own(h), slot, send_pair.at[slot], sibling).wait_send()

    @pl.loop(1, line)
    def _(d):
        @pl.loop(0, PIECES)
        def _(h):
            left_slot = (w - d * CORES) * PIECES + h
            right_slot = (w + d * CORES) * PIECES + h

            @pl.when((g - d >= 0) & ((d <= far) | (h < LENT)))
            def _():
                pl.when(has_right & ((d < far) | ((d == far) & (h < LENT))))(lambda: push(panel.at[left_slot], left_slot, send_line.at[left_slot], w + CORES).wait_send())
                push(panel.at[left_slot], left_slot, send_pair.at[left_slot], sibling).wait_send()

            @pl.when((g + d < line) & ((d <= far) | (h < LENT)))
            def _():
                pl.when(has_left & ((d < far) | ((d == far) & (h < LENT))))(lambda: push(panel.at[right_slot], right_slot, send_line.at[right_slot], w - CORES).wait_send())
                push(panel.at[right_slot], right_slot, send_pair.at[right_slot], sibling).wait_send()

    def sent(slot):
        pltpu.make_async_copy(landed.at[slot], landed.at[slot], send_sum.at[slot]).wait()

    @pl.loop(0, slots)
    def _(slot):
        pl.when(kept(slot))(lambda: sent(slot))

    @pl.when(helps)
    def _():
        @pl.loop(0, extra)
        def _(i):
            sent(slots + i)
            give_back(i).wait_send()

    pl.when(is_end)(lambda: lend().wait_send())


def on_device(wide, cols, amplitudes, integrals):
    rows_a, depth = amplitudes.shape
    rows_b = integrals.shape[0]
    share = rows_a // cols
    slots = wide * PIECES
    extra = CORES
    rows = rows_b // PIECES
    vmem = pl.BlockSpec(memory_space=pltpu.VMEM)
    return pl.pallas_call(
        functools.partial(kernel, wide, cols),
        out_shape=jax.ShapeDtypeStruct((share, wide * rows_b), jnp.float32),
        in_specs=[pl.BlockSpec(memory_space=pl.ANY)] * 2,
        out_specs=vmem,
        scratch_shapes=[
            pltpu.VMEM((rows_a, depth), jnp.float32),
            pltpu.VMEM((rows_b, depth), jnp.float32),
            pltpu.SemaphoreType.DMA((2,)),
            pltpu.VMEM((slots, rows, depth), jnp.float32),
            pltpu.VMEM((rows_a, depth), jnp.bfloat16),
            pltpu.VMEM((rows_a, depth), jnp.bfloat16),
            pltpu.VMEM((slots + extra, cols, share, rows), jnp.float32),
            pltpu.VMEM((slots + extra, cols - 1, share, rows), jnp.float32),
            pltpu.VMEM((rows_a, depth), jnp.float32),
            pltpu.VMEM((rows_a, depth), jnp.bfloat16),
            pltpu.VMEM((rows_a, depth), jnp.bfloat16),
            pltpu.VMEM((extra, share, rows), jnp.float32),
            pltpu.VMEM((extra, share, rows), jnp.float32),
            pltpu.SemaphoreType.DMA((slots + PIECES,)),
            pltpu.SemaphoreType.DMA((slots,)),
            pltpu.SemaphoreType.DMA((slots,)),
            pltpu.SemaphoreType.DMA((slots + extra,)),
            pltpu.SemaphoreType.DMA((slots + extra,)),
            pltpu.SemaphoreType.DMA,
            pltpu.SemaphoreType.DMA,
            pltpu.SemaphoreType.DMA((extra,)),
            pltpu.SemaphoreType.DMA((extra,)),
        ],
        compiler_params=pltpu.CompilerParams(
            collective_id=0, has_side_effects=True, vmem_limit_bytes=56 * 1024 * 1024),
    )(amplitudes, integrals)


def solution(mesh):
    return jax.shard_map(
        functools.partial(on_device, mesh.shape["wide"], mesh.shape["col"]),
        mesh=mesh,
        in_specs=(P("wide", "col"), P("wide", "col")),
        out_specs=P(("wide", "col"), None),
        check_vma=False,
    )
```
